32 devices in a mesh: groups: 2 (over x), mp: 16 (over z, y, core).
Axes of the slice: x: 2, y: 2, z: 4, core: 2. Of those that a mesh axis runs over, the one named last changes fastest.
Arguments:
- hidden_in: bfloat16 [1536, 2560], P(('groups', 'mp')), parts along dimension 0, may hold values from -6 to 6
- ln_gain: float32 [2560], replicated, may hold values from 0.1 to 1.9
- w_qkv: bfloat16 [3, 2560, 2048], P(None, None, 'mp'), may hold values from -2 to 2
- w_out: bfloat16 [2048, 2560], P('mp'), may hold values from -0.125 to 0.125
- residue_index: int32 [1536], P('groups'), parts along dimension 0, may hold values from 0 to 1343, as said below
- w_map: bfloat16 [32, 128], replicated, may hold values from -1 to 1, as said below
- relpos_table: float32 [65, 128], replicated, may hold values from -0.75 to 0.75
- w_side: bfloat16 [2, 2560, 128], replicated, may hold values from -0.009765625 to 0.009765625
- tri_gain: float32 [2, 128], replicated, may hold values from 0.1 to 1.9
- w_tri: bfloat16 [5, 128, 128], replicated, may hold values from -0.5 to 0.5
- w_tri_out: bfloat16 [128, 128], replicated, may hold values from -0.5 to 0.5
Outputs:
- hidden_out: bfloat16 [1536, 2560], P(('groups', 'mp')), parts along dimension 0
- pair_out: bfloat16 [1536, 768, 128], P(('groups', 'mp')), parts along dimension 0
The draws below stay inside these ranges and needn't reach their ends.
There are 2 independent parts, one for each index of `groups`. The reference program is written for one: setup_inputs(seed, part) draws one part's arguments, and reference() takes and returns one part's arrays. A program takes and returns all parts, laid end to end along the dimension named above; an argument that names none is the same for every part. Nothing has to cross between parts.
Inputs may be any that keep to these rules, and one draw needn't show every extreme that they name: `w_map`: each column sums to zero over the 32 heads before rounding to bfloat16. `residue_index`: strictly increasing from 0; consecutive entries differ by 1 or by 25, exactly 24 of them by 25.
All inputs are finite; a program needn't handle non-finite values.
Results may differ from the reference program's by a relative error of at most 0.011.
Values may be sent and summed in bfloat16 or wider, within the bound.
A program may use at most 192 MiB of HBM per device.

```python
import jax
import jax.numpy as jnp
from jax import lax

D = 2560
HEADS = 32
HD = 64
C = 128
BINS = 65
L = 768


def draw_w_qkv(key, part):
    width = HEADS * HD
    base = jnp.clip(jax.random.normal(key, (3, D, width), jnp.float32), -6.0, 6.0) * D ** (-0.5)
    factors = jnp.array([1.25, 1.25, 1.0], jnp.float32)
    stacked = base * factors[:, None, None]
    return jnp.clip(stacked, -2.0, 2.0).astype(jnp.bfloat16)


def draw_w_map(key, part):
    basis = jnp.clip(jax.random.normal(key, (HEADS, C), jnp.float32), -4.0, 4.0)
    shifted = jnp.roll(basis, 1, axis=0)
    return ((basis - shifted) * 0.05).astype(jnp.bfloat16)


def draw_residue_index(key, part):
    jump_count = L // 32
    order = jax.random.permutation(key, L - 1)
    places = order[:jump_count] + 1
    flags = jnp.zeros((L,), jnp.int32).at[places].set(1)
    increments = jnp.where(flags == 1, 25, 1)
    increments = jnp.where(jnp.arange(L) == 0, 0, increments)
    return jnp.cumsum(increments).astype(jnp.int32)


def level_of(stream_key, shape, pieces, least, largest):
    def one(position, parts):
        draws = jax.random.uniform(jax.random.fold_in(jax.random.fold_in(stream_key, 6), position), (parts,), jnp.float32, least / len(pieces), largest / len(pieces))
        return jnp.repeat(jnp.exp(draws), shape[position] // parts).reshape((-1,) + (1,) * (len(shape) - position - 1))

    gain = one(*pieces[0])
    for cut in pieces[1:]:
        gain = gain * one(*cut)
    return gain


def scatter_about(rng, dims, scale, most, split=(), kind=jnp.bfloat16):
    result = jax.random.normal(rng, dims, jnp.float32) * scale
    if len(split) > 0:
        result = level_of(rng, dims, split, -0.22, 0.18) * result
    return jnp.clip(result, min=-most, max=most).astype(kind)


def setup_inputs(seed: int = 0, part: int = 0) -> dict:
    seeds = jax.random.split(jax.random.key(seed), 12)
    own_keys = jax.random.split(jax.random.fold_in(seeds[11], part), 12)
    hidden_in = scatter_about(own_keys[0], (L, D), 1.0, 6.0, ((0, 16),))
    ln_gain = jnp.clip(1.0 + 0.18 * jax.random.normal(seeds[1], (D,), jnp.float32), 0.1, 1.9)
    w_qkv = draw_w_qkv(jax.random.fold_in(seeds[11], 71), part)
    w_out = scatter_about(seeds[3], (HEADS * HD, D), (HEADS * HD) ** -0.5, 0.125, ((0, 16),))
    residue_index = draw_residue_index(jax.random.fold_in(jax.random.fold_in(seeds[11], part), 71), part)
    w_map = draw_w_map(jax.random.fold_in(seeds[11], 71), part)
    relpos_table = scatter_about(seeds[6], (BINS, C), 0.12, 0.75, (), jnp.float32)
    w_side = scatter_about(seeds[7], (2, D, C), (128 * D) ** -0.5, 0.009765625)
    tri_gain = jnp.clip(1.0 + 0.18 * jax.random.normal(seeds[8], (2, C), jnp.float32), 0.1, 1.9)
    w_tri = scatter_about(seeds[9], (5, C, C), C ** -0.5, 0.5)
    w_tri_out = scatter_about(seeds[10], (C, C), C ** -0.5, 0.5)
    return dict(hidden_in=hidden_in, ln_gain=ln_gain, w_qkv=w_qkv, w_out=w_out, residue_index=residue_index, w_map=w_map, relpos_table=relpos_table, w_side=w_side, tri_gain=tri_gain, w_tri=w_tri, w_tri_out=w_tri_out)


def layer_norm(tensor, gain_vec, norm_axis):
    center = lax.optimization_barrier(jnp.mean(tensor, axis=norm_axis, keepdims=True))
    centered = tensor - center
    variance = lax.optimization_barrier(jnp.mean(centered * centered, axis=norm_axis, keepdims=True))
    return centered * lax.rsqrt(variance + 1e-05) * gain_vec

def rotary_tables(length, width):
    inv_freq = 1.0 / 10000.0 ** (jnp.arange(0, width, 2, dtype=jnp.float32) / width)
    angles = jnp.arange(length, dtype=jnp.float32)[:, None] * inv_freq[None, :]
    angles = jnp.concatenate([angles, angles], axis=-1)
    return (jnp.cos(angles)[:, None, :], jnp.sin(angles)[:, None, :])

def rotate(tensor, cos_table, sin_table):
    middle = tensor.shape[-1] // 2
    turned = jnp.concatenate([-tensor[..., middle:], tensor[..., :middle]], axis=-1)
    return tensor * cos_table + turned * sin_table

def gated_edge(pair_normed, w_value, w_gate):
    value_part = jnp.einsum('ijc,cd->dij', pair_normed.astype(jnp.float32), w_value.astype(jnp.float32))
    gate_part = jnp.einsum('ijc,cd->dij', pair_normed.astype(jnp.float32), w_gate.astype(jnp.float32))
    return (jax.nn.sigmoid(gate_part) * value_part).astype(jnp.bfloat16)

def reference(hidden_in, ln_gain, w_qkv, w_out, residue_index, w_map, relpos_table, w_side, tri_gain, w_tri, w_tri_out):
    length = hidden_in.shape[0]
    normed = layer_norm(hidden_in.astype(jnp.float32), ln_gain, -1).astype(jnp.bfloat16)
    projected = jnp.einsum('rd,tdh->trh', normed.astype(jnp.float32), w_qkv.astype(jnp.float32))
    projected = projected.reshape(3, length, HEADS, HD)
    cos_table, sin_table = rotary_tables(length, HD)
    queries = rotate(projected[0] * HD ** (-0.5), cos_table, sin_table).astype(jnp.bfloat16)
    key_rows = rotate(projected[1], cos_table, sin_table).astype(jnp.bfloat16)
    value_rows = projected[2].astype(jnp.bfloat16)
    scores = jnp.einsum('qhd,khd->hqk', queries.astype(jnp.float32), key_rows.astype(jnp.float32))
    attn_probs = jax.nn.softmax(scores, axis=-1).astype(jnp.bfloat16)
    attended = jnp.einsum('hqk,khd->qhd', attn_probs.astype(jnp.float32), value_rows.astype(jnp.float32))
    attended = attended.astype(jnp.bfloat16).reshape(length, HEADS * HD)
    hidden_out = (hidden_in.astype(jnp.float32) + jnp.dot(attended, w_out, preferred_element_type=jnp.float32)).astype(jnp.bfloat16)
    pair_sum = length * jnp.einsum('hij,hc->ijc', attn_probs.astype(jnp.float32), w_map.astype(jnp.float32))
    reach = (BINS - 1) // 2
    rel_bins = jnp.clip(residue_index[None, :] - residue_index[:, None], -reach, reach) + reach
    pair_sum = pair_sum + relpos_table[rel_bins.astype(jnp.int32)]
    left_terms = jnp.dot(hidden_out, w_side[0], preferred_element_type=jnp.float32).astype(jnp.bfloat16)
    right_terms = jnp.dot(hidden_out, w_side[1], preferred_element_type=jnp.float32).astype(jnp.bfloat16)
    pair_sum = pair_sum + left_terms[:, None, :].astype(jnp.float32) + right_terms[None, :, :].astype(jnp.float32)
    pair_normed = layer_norm(pair_sum, tri_gain[0], -1).astype(jnp.bfloat16)
    left_edge = gated_edge(pair_normed, w_tri[0], w_tri[1])
    right_edge = gated_edge(pair_normed, w_tri[2], w_tri[3])
    out_gate = jax.nn.sigmoid(jnp.einsum('ijc,cd->ijd', pair_normed.astype(jnp.float32), w_tri[4].astype(jnp.float32)))
    products = jnp.einsum('cik,cjk->cij', left_edge.astype(jnp.float32), right_edge.astype(jnp.float32)).astype(jnp.bfloat16)
    prod_normed = layer_norm(products.astype(jnp.float32), tri_gain[1][:, None, None], 0).astype(jnp.bfloat16)
    projected_out = jnp.einsum('cij,cd->ijd', prod_normed.astype(jnp.float32), w_tri_out.astype(jnp.float32))
    pair_out = (pair_sum + out_gate * projected_out).astype(jnp.bfloat16)
    return (hidden_out, pair_out)
```

```python
import functools

import jax
import jax.numpy as jnp
from jax import lax
from jax.experimental import pallas as pl
from jax.experimental.pallas import tpu as pltpu
from jax.sharding import PartitionSpec as P

HD = 64
BINS = 65
BIN_ROWS = 80
LANES = 128
CHUNKS = 3
VMEM_BYTES = 60 * 1024 * 1024


def layer_norm(tensor, gain_vec, norm_axis):
    center = jnp.mean(tensor, axis=norm_axis, keepdims=True)
    centered = tensor - center
    variance = jnp.mean(centered * centered, axis=norm_axis, keepdims=True)
    return centered * lax.rsqrt(variance + 1e-05) * gain_vec


def rotary_tables(length, width):
    inv_freq = 1.0 / 10000.0 ** (jnp.arange(0, width, 2, dtype=jnp.float32) / width)
    angles = jnp.arange(length, dtype=jnp.float32)[:, None] * inv_freq[None, :]
    angles = jnp.concatenate([angles, angles], axis=-1)
    return (jnp.cos(angles)[:, None, :], jnp.sin(angles)[:, None, :])


def rotate(tensor, cos_table, sin_table):
    middle = tensor.shape[-1] // 2
    turned = jnp.concatenate([-tensor[..., middle:], tensor[..., :middle]], axis=-1)
    return tensor * cos_table + turned * sin_table


def two_terms(value):
    high = lax.reduce_precision(value, 8, 7)
    return high.astype(jnp.bfloat16), (value - high).astype(jnp.bfloat16)


def maps_kernel(q_ref, k_ref, out_ref, scratch):
    heads, rows, _ = q_ref.shape
    blocks = scratch.shape[0]

    def one_head(h, carry):
        scores = jnp.dot(q_ref[h], k_ref[h], preferred_element_type=jnp.float32)
        top = jnp.max(scores, axis=-1, keepdims=True)
        powers = jnp.exp(scores - top)
        probs = powers / jnp.sum(powers, axis=-1, keepdims=True)
        start = pl.multiple_of(h * rows, 8)
        for n in range(blocks):
            scratch[n, pl.ds(start, rows), :] = probs[:, n * LANES : (n + 1) * LANES]
        return carry

    lax.fori_loop(0, heads, one_head, 0, unroll=2)

    def one_row(j, carry):
        for n in range(blocks):
            rows_of = scratch[n, pl.ds(j, heads, stride=rows), :]
            out_ref[j, :, n * LANES : (n + 1) * LANES] = rows_of.astype(jnp.bfloat16)
        return carry

    lax.fori_loop(0, rows, one_row, 0, unroll=2)


def attention_maps(queries, keys, block):
    heads, rows, width = queries.shape
    length = keys.shape[2]
    return pl.pallas_call(
        maps_kernel,
        out_shape=jax.ShapeDtypeStruct((rows, heads, length), jnp.bfloat16),
        grid=(rows // block,),
        in_specs=[
            pl.BlockSpec((heads, block, width), lambda b: (0, b, 0)),
            pl.BlockSpec((heads, width, length), lambda b: (0, 0, 0)),
        ],
        out_specs=pl.BlockSpec((block, heads, length), lambda b: (b, 0, 0)),
        scratch_shapes=[pltpu.VMEM((length // LANES, heads * block, LANES), jnp.float32)],
        compiler_params=pltpu.CompilerParams(vmem_limit_bytes=VMEM_BYTES),
        cost_estimate=pl.CostEstimate(
            flops=2 * heads * rows * length * width * 4,
            bytes_accessed=2 * heads * rows * length,
            transcendentals=heads * rows * length,
        ),
        name="attention_maps",
    )(queries, keys)


def edges_kernel(own, row_index, maps_ref, mix_ref, right_ref, gain_ref, w_ref, cols_ref, *rest):
    scratch = rest[-1]
    block, heads, length = maps_ref.shape
    channels = right_ref.shape[0]
    width = gain_ref.shape[1]
    eye_rows = mix_ref.shape[2] - 2 * heads - 2 * BIN_ROWS
    reach = (BINS - 1) // 2
    first = pl.program_id(0) * block

    def one_row(j, carry):
        here = row_index[first + j]
        place = lax.broadcasted_iota(jnp.int32, (eye_rows, width), 0)
        eye = jnp.where(place == j, 1.0, 0.0).astype(jnp.bfloat16)
        for n in range(length // width):
            cols = slice(n * width, (n + 1) * width)
            bins = jnp.clip(cols_ref[:, cols] - here, -reach, reach) + reach
            places = lax.broadcasted_iota(jnp.int32, (BIN_ROWS, width), 0)
            hot = jnp.where(places == bins, 1.0, 0.0).astype(jnp.bfloat16)
            probs = maps_ref[j, :, cols]
            terms = jnp.concatenate([probs, probs, eye, hot, hot], axis=0)
            pair = jnp.dot(mix_ref[0], terms, preferred_element_type=jnp.float32)
            pair = pair + right_ref[:, cols]
            center = jnp.sum(pair, axis=0, keepdims=True) * (1.0 / channels)
            centered = pair - center
            variance = jnp.sum(centered * centered, axis=0, keepdims=True) * (1.0 / channels)
            normed = centered * lax.rsqrt(variance + 1e-05) * gain_ref[...]
            gated = jnp.dot(
                w_ref[...], normed.astype(jnp.bfloat16), preferred_element_type=jnp.float32
            )
            value = gated[:channels]
            edge = value + value * jnp.tanh(gated[channels : 2 * channels])
            start = pl.multiple_of(j * channels, 8)
            for m in range(width // LANES):
                scratch[n * (width // LANES) + m, pl.ds(start, channels), :] = edge[
                    :, m * LANES : (m + 1) * LANES
                ]
            if own:
                rest[2][j, :, cols] = pair
                rest[3][j, :, cols] = (0.5 + 0.5 * jnp.tanh(gated[2 * channels :])).astype(
                    jnp.bfloat16
                )
        return carry

    lax.fori_loop(0, block, one_row, 0)
    half = channels // 2

    def one_channel(c, carry):
        for n in range(length // LANES):
            for side in range(2):
                rows_of = scratch[n, pl.ds(c + side * half, block, stride=channels), :]
                rest[side][c, :, n * LANES : (n + 1) * LANES] = rows_of.astype(jnp.bfloat16)
        return carry

    lax.fori_loop(0, half, one_channel, 0, unroll=2)


def edges(own, row_index, maps, mix, right, gain, weights, cols, block, skip=0, rows=None):
    _, heads, length = maps.shape
    rows = maps.shape[0] if rows is None else rows
    channels = right.shape[0]
    half = channels // 2
    out_shape = [jax.ShapeDtypeStruct((half, rows, length), jnp.bfloat16)] * 2
    out_specs = [pl.BlockSpec((half, block, length), lambda b, s: (0, b, 0))] * 2
    if own:
        out_shape += [
            jax.ShapeDtypeStruct((rows, channels, length), jnp.float32),
            jax.ShapeDtypeStruct((rows, channels, length), jnp.bfloat16),
        ]
        out_specs += [pl.BlockSpec((block, channels, length), lambda b, s: (b, 0, 0))] * 2
    first = skip // block
    return pl.pallas_call(
        functools.partial(edges_kernel, own),
        out_shape=out_shape,
        grid_spec=pltpu.PrefetchScalarGridSpec(
            num_scalar_prefetch=1,
            grid=(rows // block,),
            in_specs=[
                pl.BlockSpec((block, heads, length), lambda b, s: (b + first, 0, 0)),
                pl.BlockSpec((1,) + mix.shape[1:], lambda b, s: (b, 0, 0)),
                pl.BlockSpec(right.shape, lambda b, s: (0, 0)),
                pl.BlockSpec(gain.shape, lambda b, s: (0, 0)),
                pl.BlockSpec(weights.shape, lambda b, s: (0, 0)),
                pl.BlockSpec(cols.shape, lambda b, s: (0, 0)),
            ],
            out_specs=out_specs,
            scratch_shapes=[pltpu.VMEM((length // LANES, block * channels, LANES), jnp.float32)],
        ),
        compiler_params=pltpu.CompilerParams(vmem_limit_bytes=VMEM_BYTES),
        cost_estimate=pl.CostEstimate(
            flops=2 * rows * length * channels * 800,
            bytes_accessed=2 * rows * length * channels,
            transcendentals=rows * length * channels,
        ),
        name="own_edges" if own else "right_edges",
    )(row_index, maps, mix, right, gain, weights, cols)


def final_kernel(core, mine_ref, theirs_ref, pair_ref, gate_ref, gain_ref, w_ref, out_ref, scratch):
    half, block, width = mine_ref.shape[1:]
    for n, ref in enumerate((mine_ref, theirs_ref)):

        def one_channel(c, carry):
            start = pl.multiple_of(c * block, 8)
            scratch[n, pl.ds(start, block), :] = ref[0, c].astype(jnp.float32)
            return carry

        lax.fori_loop(0, half, one_channel, 0, unroll=4)

    def one_row(i, carry):
        products = jnp.concatenate(
            [scratch[n, pl.ds(i, half, stride=block), :] for n in range(2)], axis=0
        )
        center = jnp.mean(products, axis=0, keepdims=True)
        centered = products - center
        variance = jnp.mean(centered * centered, axis=0, keepdims=True)
        normed = (centered * lax.rsqrt(variance + 1e-05) * gain_ref[...]).astype(jnp.bfloat16)
        projected = jnp.dot(w_ref[...], normed, preferred_element_type=jnp.float32)
        total = pair_ref[i] + gate_ref[i].astype(jnp.float32) * projected
        out_ref[i] = total.T.astype(jnp.bfloat16)
        return carry

    lax.fori_loop(0, block, one_row, 0, unroll=2)


def finish(core, mine, theirs, pair, gate, gain, weights, block):
    pieces, half, rows, width = mine.shape
    _, channels, length = pair.shape
    each = pieces // 2

    def column(u, core):
        side = u // each
        return (side + core[0] - 2 * side * core[0]) * each + u % each

    return pl.pallas_call(
        final_kernel,
        out_shape=jax.ShapeDtypeStruct((rows, length, channels), jnp.bfloat16),
        grid_spec=pltpu.PrefetchScalarGridSpec(
            num_scalar_prefetch=1,
            grid=(rows // block, pieces),
            in_specs=[
                pl.BlockSpec((1, half, block, width), lambda b, u, s: (u, 0, b, 0)),
                pl.BlockSpec(
                    (1, half, block, width), lambda b, u, s: ((u + each) % pieces, 0, b, 0)
                ),
                pl.BlockSpec((block, channels, width), lambda b, u, s: (b, 0, column(u, s))),
                pl.BlockSpec((block, channels, width), lambda b, u, s: (b, 0, column(u, s))),
                pl.BlockSpec(gain.shape, lambda b, u, s: (0, 0)),
                pl.BlockSpec(weights.shape, lambda b, u, s: (0, 0)),
            ],
            out_specs=pl.BlockSpec((block, width, channels), lambda b, u, s: (b, column(u, s), 0)),
            scratch_shapes=[pltpu.VMEM((2, half * block, width), jnp.float32)],
        ),
        compiler_params=pltpu.CompilerParams(vmem_limit_bytes=VMEM_BYTES),
        name="finish",
    )(core, mine, theirs, pair, gate, gain, weights)


def per_device(
    hidden_in,
    ln_gain,
    w_qkv,
    w_out,
    residue_index,
    w_map,
    relpos_table,
    w_side,
    tri_gain,
    w_tri,
    w_tri_out,
):
    local_rows = hidden_in.shape[0]
    devices_mp = lax.axis_size("mp")
    me = lax.axis_index("mp")
    core = lax.rem(me, 2)
    length = local_rows * devices_mp
    local_heads = w_qkv.shape[2] // HD
    heads, channels = w_map.shape
    swap = [(d, d ^ 1) for d in range(devices_mp)]
    normed = layer_norm(hidden_in.astype(jnp.float32), ln_gain, -1).astype(jnp.bfloat16)
    projected = jnp.einsum(
        "rd,tdh->trh",
        lax.all_gather(normed, "mp", axis=0, tiled=True),
        w_qkv,
        preferred_element_type=jnp.float32,
    )
    projected = projected.reshape(3, length, local_heads, HD)
    cos_table, sin_table = rotary_tables(length, HD)
    queries = rotate(projected[0] * HD ** (-0.5), cos_table, sin_table).astype(jnp.bfloat16)
    key_rows = rotate(projected[1], cos_table, sin_table).astype(jnp.bfloat16)
    value_rows = projected[2].astype(jnp.bfloat16)
    both = jnp.stack([queries.reshape(length, -1).T, key_rows.reshape(length, -1).T])
    gathered = lax.all_gather(both, "mp", axis=1, tiled=True)
    all_keys = gathered[1].reshape(heads, HD, length)
    all_queries = gathered[0].reshape(heads, HD, length).transpose(0, 2, 1)

    scores = jnp.einsum("qhd,khd->hqk", queries, key_rows, preferred_element_type=jnp.float32)
    attn_probs = jax.nn.softmax(scores, axis=-1).astype(jnp.bfloat16)
    attended = jnp.einsum(
        "hqk,khd->qhd", attn_probs, value_rows, preferred_element_type=jnp.float32
    )
    attended = attended.astype(jnp.bfloat16).reshape(length, local_heads * HD)
    mixed = lax.psum_scatter(
        jnp.dot(attended, w_out, preferred_element_type=jnp.float32).astype(jnp.bfloat16),
        "mp",
        scatter_dimension=0,
        tiled=True,
    ).astype(jnp.float32)
    hidden_out = (hidden_in.astype(jnp.float32) + mixed).astype(jnp.bfloat16)

    half_rows = length // 2
    row_start = me * local_rows
    half_start = core * half_rows
    own_maps = attention_maps(
        lax.dynamic_slice_in_dim(all_queries, row_start, local_rows, 1), all_keys, local_rows
    )
    map_block = 64 if half_rows % 64 == 0 else local_rows
    half_maps = attention_maps(
        lax.dynamic_slice_in_dim(all_queries, half_start, half_rows, 1), all_keys, map_block
    )

    side_terms = jnp.einsum(
        "rd,sdc->src", hidden_out, w_side, preferred_element_type=jnp.float32
    ).astype(jnp.bfloat16)
    all_sides = lax.all_gather(side_terms, "mp", axis=1, tiled=True)
    left_rows = all_sides[0]
    right = all_sides[1].astype(jnp.float32).T

    map_high, map_low = two_terms(w_map.astype(jnp.float32) * length)
    bin_high, bin_low = two_terms(relpos_table)
    bin_pad = ((0, BIN_ROWS - relpos_table.shape[0]), (0, 0))

    def mixing(left, block):
        count = left.shape[0] // block
        eye_rows = -(-block // 16) * 16
        lefts = jnp.pad(left.reshape(count, block, channels), ((0, 0), (0, eye_rows - block), (0, 0)))
        parts = [map_high, map_low, lefts, jnp.pad(bin_high, bin_pad), jnp.pad(bin_low, bin_pad)]
        parts = [jnp.broadcast_to(p, (count,) + p.shape[-2:]) for p in parts]
        return jnp.concatenate(parts, axis=1).transpose(0, 2, 1)

    turn = -core * (channels // 2)
    gain = jnp.broadcast_to(tri_gain[0][:, None], (channels, 2 * LANES))
    halved = w_tri * jnp.asarray(0.5, w_tri.dtype)
    right_w = jnp.concatenate([jnp.roll(halved[p].T, turn, axis=0) for p in (2, 3)], axis=0)
    left_w = jnp.concatenate(
        [jnp.roll(halved[p].T, turn, axis=0) for p in (0, 1)] + [halved[4].T], axis=0
    )
    cols = residue_index[None, :]

    block = 16 if local_rows % 16 == 0 else local_rows
    half_left = lax.dynamic_slice_in_dim(left_rows, half_start, half_rows, 0)
    half_index = lax.dynamic_slice_in_dim(residue_index, half_start, half_rows, 0)
    each = half_rows // CHUNKS
    kept, arriving = [], []
    r_block = 16 if each % 16 == 0 else each
    for n in range(CHUNKS):
        part = slice(n * each, (n + 1) * each)
        keep, send = edges(
            False,
            half_index[part],
            half_maps,
            mixing(half_left[part], r_block),
            right,
            gain,
            right_w,
            cols,
            r_block,
            n * each,
            each,
        )
        kept.append(keep)
        arriving.append(lax.ppermute(send, "mp", swap))
    left_keep, left_send, pair, gate = edges(
        True,
        lax.dynamic_slice_in_dim(residue_index, row_start, local_rows, 0),
        own_maps,
        mixing(lax.dynamic_slice_in_dim(left_rows, row_start, local_rows, 0), block),
        right,
        gain,
        left_w,
        cols,
        block,
    )
    lefts = jnp.concatenate([left_keep, lax.ppermute(left_send, "mp", swap)], axis=1)
    products = jnp.stack(
        [
            jnp.einsum("cik,cjk->cij", lefts, part, preferred_element_type=jnp.float32).astype(
                jnp.bfloat16
            )
            for part in kept + arriving
        ]
    )
    mine = products[:, :, :local_rows]
    theirs = lax.ppermute(products[:, :, local_rows:], "mp", swap)
    pair_out = finish(
        core[None],
        mine,
        theirs,
        pair,
        gate,
        jnp.broadcast_to(jnp.roll(tri_gain[1], turn)[:, None], (channels, each)),
        jnp.roll(w_tri_out, turn, axis=0).T,
        block,
    )
    return (hidden_out, pair_out)


def solution(mesh):
    placed = (
        P(("groups", "mp"), None),
        P(),
        P(None, None, "mp"),
        P("mp", None),
        P("groups"),
        P(),
        P(),
        P(),
        P(),
        P(),
        P(),
    )
    return jax.shard_map(
        per_device,
        mesh=mesh,
        in_specs=placed,
        out_specs=(P(("groups", "mp"), None), P(("groups", "mp"), None, None)),
        check_vma=False,
    )
```

```python
import functools

import jax
import jax.numpy as jnp
from jax import lax
from jax.experimental import pallas as pl
from jax.experimental.pallas import tpu as pltpu
from jax.sharding import PartitionSpec as P

HD = 64
BINS = 65
BIN_ROWS = 80
LANES = 128
CHUNKS = 3
PAD = 8
VMEM_BYTES = 60 * 1024 * 1024


def layer_norm(tensor, gain_vec, norm_axis):
    center = jnp.mean(tensor, axis=norm_axis, keepdims=True)
    centered = tensor - center
    variance = jnp.mean(centered * centered, axis=norm_axis, keepdims=True)
    return centered * lax.rsqrt(variance + 1e-05) * gain_vec


def rotary_tables(length, width):
    inv_freq = 1.0 / 10000.0 ** (jnp.arange(0, width, 2, dtype=jnp.float32) / width)
    angles = jnp.arange(length, dtype=jnp.float32)[:, None] * inv_freq[None, :]
    angles = jnp.concatenate([angles, angles], axis=-1)
    return (jnp.cos(angles)[:, None, :], jnp.sin(angles)[:, None, :])


def rotate(tensor, cos_table, sin_table):
    middle = tensor.shape[-1] // 2
    turned = jnp.concatenate([-tensor[..., middle:], tensor[..., :middle]], axis=-1)
    return tensor * cos_table + turned * sin_table


def two_terms(value):
    high = lax.reduce_precision(value, 8, 7)
    return high.astype(jnp.bfloat16), (value - high).astype(jnp.bfloat16)


def maps_kernel(q_ref, k_ref, out_ref, scratch):
    heads, rows, _ = q_ref.shape
    blocks = scratch.shape[0]

    def one_head(h, carry):
        scores = jnp.dot(q_ref[h], k_ref[h], preferred_element_type=jnp.float32)
        top = jnp.max(scores, axis=-1, keepdims=True)
        powers = jnp.exp(scores - top)
        probs = powers / jnp.sum(powers, axis=-1, keepdims=True)
        start = pl.multiple_of(h * (rows + PAD), 8)
        for n in range(blocks):
            scratch[n, pl.ds(start, rows), :] = probs[:, n * LANES : (n + 1) * LANES]
        return carry

    lax.fori_loop(0, heads, one_head, 0, unroll=8)

    def one_row(j, carry):
        for n in range(blocks):
            rows_of = scratch[n, pl.ds(j, heads, stride=rows + PAD), :]
            out_ref[j, :, n * LANES : (n + 1) * LANES] = rows_of.astype(jnp.bfloat16)
        return carry

    lax.fori_loop(0, rows, one_row, 0, unroll=8)


def attention_maps(queries, keys, block):
    heads, rows, width = queries.shape
    length = keys.shape[2]
    return pl.pallas_call(
        maps_kernel,
        out_shape=jax.ShapeDtypeStruct((rows, heads, length), jnp.bfloat16),
        grid=(rows // block,),
        in_specs=[
            pl.BlockSpec((heads, block, width), lambda b: (0, b, 0)),
            pl.BlockSpec((heads, width, length), lambda b: (0, 0, 0)),
        ],
        out_specs=pl.BlockSpec((block, heads, length), lambda b: (b, 0, 0)),
        scratch_shapes=[pltpu.VMEM((length // LANES, heads * (block + PAD), LANES), jnp.float32)],
        compiler_params=pltpu.CompilerParams(vmem_limit_bytes=VMEM_BYTES),
        cost_estimate=pl.CostEstimate(
            flops=2 * heads * rows * length * width * 4,
            bytes_accessed=2 * heads * rows * length,
            transcendentals=heads * rows * length,
        ),
        name="attention_maps",
    )(queries, keys)


def edges_kernel(own, row_index, maps_ref, mix_ref, right_ref, gain_ref, w_ref, cols_ref, *rest):
    scratch = rest[-1]
    block, heads, length = maps_ref.shape
    channels = right_ref.shape[0]
    width = gain_ref.shape[1]
    eye_rows = mix_ref.shape[2] - 2 * heads - 2 * BIN_ROWS
    reach = (BINS - 1) // 2
    first = pl.program_id(0) * block

    def one_row(j, carry):
        here = row_index[first + j]
        place = lax.broadcasted_iota(jnp.int32, (eye_rows, width), 0)
        eye = jnp.where(place == j, 1.0, 0.0).astype(jnp.bfloat16)
        for n in range(length // width):
            cols = slice(n * width, (n + 1) * width)
            bins = jnp.clip(cols_ref[:, cols] - here, -reach, reach) + reach
            places = lax.broadcasted_iota(jnp.int32, (BIN_ROWS, width), 0)
            hot = jnp.where(places == bins, 1.0, 0.0).astype(jnp.bfloat16)
            probs = maps_ref[j, :, cols]
            terms = jnp.concatenate([probs, probs, eye, hot, hot], axis=0)
            pair = jnp.dot(mix_ref[0], terms, preferred_element_type=jnp.float32)
            pair = pair + right_ref[:, cols]
            center = jnp.sum(pair, axis=0, keepdims=True) * (1.0 / channels)
            centered = pair - center
            variance = jnp.sum(centered * centered, axis=0, keepdims=True) * (1.0 / channels)
            normed = centered * lax.rsqrt(variance + 1e-05) * gain_ref[...]
            gated = jnp.dot(
                w_ref[...], normed.astype(jnp.bfloat16), preferred_element_type=jnp.float32
            )
            value = gated[:channels]
            edge = value + value * jnp.tanh(gated[channels : 2 * channels])
            start = pl.multiple_of(j * (channels + PAD), 8)
            for m in range(width // LANES):
                scratch[n * (width // LANES) + m, pl.ds(start, channels), :] = edge[
                    :, m * LANES : (m + 1) * LANES
                ]
            if own:
                rest[2][j, :, cols] = pair
                rest[3][j, :, cols] = (0.5 + 0.5 * jnp.tanh(gated[2 * channels :])).astype(
                    jnp.bfloat16
                )
        return carry

    lax.fori_loop(0, block, one_row, 0, unroll=8)
    half = channels // 2

    def one_channel(c, carry):
        for n in range(length // LANES):
            for side in range(2):
                rows_of = scratch[n, pl.ds(c + side * half, block, stride=channels + PAD), :]
                rest[side][c, :, n * LANES : (n + 1) * LANES] = rows_of.astype(jnp.bfloat16)
        return carry

    lax.fori_loop(0, half, one_channel, 0, unroll=16)


def edges(own, row_index, maps, mix, right, gain, weights, cols, block, skip=0, rows=None):
    _, heads, length = maps.shape
    rows = maps.shape[0] if rows is None else rows
    channels = right.shape[0]
    half = channels // 2
    out_shape = [jax.ShapeDtypeStruct((half, rows, length), jnp.bfloat16)] * 2
    out_specs = [pl.BlockSpec((half, block, length), lambda b, s: (0, b, 0))] * 2
    if own:
        out_shape += [
            jax.ShapeDtypeStruct((rows, channels, length), jnp.float32),
            jax.ShapeDtypeStruct((rows, channels, length), jnp.bfloat16),
        ]
        out_specs += [pl.BlockSpec((block, channels, length), lambda b, s: (b, 0, 0))] * 2
    first = skip // block
    return pl.pallas_call(
        functools.partial(edges_kernel, own),
        out_shape=out_shape,
        grid_spec=pltpu.PrefetchScalarGridSpec(
            num_scalar_prefetch=1,
            grid=(rows // block,),
            in_specs=[
                pl.BlockSpec((block, heads, length), lambda b, s: (b + first, 0, 0)),
                pl.BlockSpec((1,) + mix.shape[1:], lambda b, s: (b, 0, 0)),
                pl.BlockSpec(right.shape, lambda b, s: (0, 0)),
                pl.BlockSpec(gain.shape, lambda b, s: (0, 0)),
                pl.BlockSpec(weights.shape, lambda b, s: (0, 0)),
                pl.BlockSpec(cols.shape, lambda b, s: (0, 0)),
            ],
            out_specs=out_specs,
            scratch_shapes=[pltpu.VMEM((length // LANES, block * (channels + PAD), LANES), jnp.float32)],
        ),
        compiler_params=pltpu.CompilerParams(vmem_limit_bytes=VMEM_BYTES),
        cost_estimate=pl.CostEstimate(
            flops=2 * rows * length * channels * 800,
            bytes_accessed=2 * rows * length * channels,
            transcendentals=rows * length * channels,
        ),
        name="own_edges" if own else "right_edges",
    )(row_index, maps, mix, right, gain, weights, cols)


def final_kernel(core, mine_ref, theirs_ref, pair_ref, gate_ref, gain_ref, w_ref, out_ref, scratch):
    half, block, width = mine_ref.shape[1:]
    for n, ref in enumerate((mine_ref, theirs_ref)):

        def one_channel(c, carry):
            start = pl.multiple_of(c * (block + PAD), 8)
            scratch[n, pl.ds(start, block), :] = ref[0, c].astype(jnp.float32)
            return carry

        lax.fori_loop(0, half, one_channel, 0, unroll=8)

    def one_row(i, carry):
        products = jnp.concatenate(
            [scratch[n, pl.ds(i, half, stride=block + PAD), :] for n in range(2)], axis=0
        )
        center = jnp.mean(products, axis=0, keepdims=True)
        centered = products - center
        variance = jnp.mean(centered * centered, axis=0, keepdims=True)
        normed = (centered * lax.rsqrt(variance + 1e-05) * gain_ref[...]).astype(jnp.bfloat16)
        projected = jnp.dot(w_ref[...], normed, preferred_element_type=jnp.float32)
        total = pair_ref[i] + gate_ref[i].astype(jnp.float32) * projected
        out_ref[i] = total.T.astype(jnp.bfloat16)
        return carry

    lax.fori_loop(0, block, one_row, 0, unroll=16)


def finish(core, mine, theirs, pair, gate, gain, weights, block):
    pieces, half, rows, width = mine.shape
    _, channels, length = pair.shape
    each = pieces // 2

    def column(u, core):
        side = u // each
        return (side + core[0] - 2 * side * core[0]) * each + u % each

    return pl.pallas_call(
        final_kernel,
        out_shape=jax.ShapeDtypeStruct((rows, length, channels), jnp.bfloat16),
        grid_spec=pltpu.PrefetchScalarGridSpec(
            num_scalar_prefetch=1,
            grid=(rows // block, pieces),
            in_specs=[
                pl.BlockSpec((1, half, block, width), lambda b, u, s: (u, 0, b, 0)),
                pl.BlockSpec(
                    (1, half, block, width), lambda b, u, s: ((u + each) % pieces, 0, b, 0)
                ),
                pl.BlockSpec((block, channels, width), lambda b, u, s: (b, 0, column(u, s))),
                pl.BlockSpec((block, channels, width), lambda b, u, s: (b, 0, column(u, s))),
                pl.BlockSpec(gain.shape, lambda b, u, s: (0, 0)),
                pl.BlockSpec(weights.shape, lambda b, u, s: (0, 0)),
            ],
            out_specs=pl.BlockSpec((block, width, channels), lambda b, u, s: (b, column(u, s), 0)),
            scratch_shapes=[pltpu.VMEM((2, half * (block + PAD), width), jnp.float32)],
        ),
        compiler_params=pltpu.CompilerParams(vmem_limit_bytes=VMEM_BYTES),
        name="finish",
    )(core, mine, theirs, pair, gate, gain, weights)


def per_device(
    hidden_in,
    ln_gain,
    w_qkv,
    w_out,
    residue_index,
    w_map,
    relpos_table,
    w_side,
    tri_gain,
    w_tri,
    w_tri_out,
):
    local_rows = hidden_in.shape[0]
    devices_mp = lax.axis_size("mp")
    me = lax.axis_index("mp")
    core = lax.rem(me, 2)
    length = local_rows * devices_mp
    local_heads = w_qkv.shape[2] // HD
    heads, channels = w_map.shape
    swap = [(d, d ^ 1) for d in range(devices_mp)]
    normed = layer_norm(hidden_in.astype(jnp.float32), ln_gain, -1).astype(jnp.bfloat16)
    projected = jnp.einsum(
        "rd,tdh->trh",
        lax.all_gather(normed, "mp", axis=0, tiled=True),
        w_qkv,
        preferred_element_type=jnp.float32,
    )
    projected = projected.reshape(3, length, local_heads, HD)
    cos_table, sin_table = rotary_tables(length, HD)
    queries = rotate(projected[0] * HD ** (-0.5), cos_table, sin_table).astype(jnp.bfloat16)
    key_rows = rotate(projected[1], cos_table, sin_table).astype(jnp.bfloat16)
    value_rows = projected[2].astype(jnp.bfloat16)
    both = jnp.stack([queries.reshape(length, -1).T, key_rows.reshape(length, -1).T])
    gathered = lax.all_gather(both, "mp", axis=1, tiled=True)

    scores = jnp.einsum("qhd,khd->hqk", queries, key_rows, preferred_element_type=jnp.float32)
    attn_probs = jax.nn.softmax(scores, axis=-1).astype(jnp.bfloat16)
    attended = jnp.einsum(
        "hqk,khd->qhd", attn_probs, value_rows, preferred_element_type=jnp.float32
    )
    attended = attended.astype(jnp.bfloat16).reshape(length, local_heads * HD)
    partial, gathered = lax.optimization_barrier(
        (
            jnp.dot(attended, w_out, preferred_element_type=jnp.float32).astype(jnp.bfloat16),
            gathered,
        )
    )
    all_keys = gathered[1].reshape(heads, HD, length)
    all_queries = gathered[0].reshape(heads, HD, length).transpose(0, 2, 1)
    mixed = lax.psum_scatter(partial, "mp", scatter_dimension=0, tiled=True)

    half_rows = length // 2
    row_start = me * local_rows
    half_start = core * half_rows
    own_maps = attention_maps(
        lax.dynamic_slice_in_dim(all_queries, row_start, local_rows, 1), all_keys, local_rows
    )
    map_block = 64 if half_rows % 64 == 0 else local_rows
    half_maps = attention_maps(
        lax.dynamic_slice_in_dim(all_queries, half_start, half_rows, 1), all_keys, map_block
    )

    mixed, own_maps, half_maps = lax.optimization_barrier((mixed, own_maps, half_maps))
    hidden_out = (hidden_in.astype(jnp.float32) + mixed.astype(jnp.float32)).astype(jnp.bfloat16)
    side_terms = jnp.einsum(
        "rd,sdc->src", hidden_out, w_side, preferred_element_type=jnp.float32
    ).astype(jnp.bfloat16)
    all_sides = lax.all_gather(side_terms, "mp", axis=1, tiled=True)
    left_rows = all_sides[0]
    right = all_sides[1].astype(jnp.float32).T

    map_high, map_low = two_terms(w_map.astype(jnp.float32) * length)
    bin_high, bin_low = two_terms(relpos_table)
    bin_pad = ((0, BIN_ROWS - relpos_table.shape[0]), (0, 0))

    def mixing(left, block):
        count = left.shape[0] // block
        eye_rows = -(-block // 16) * 16
        lefts = jnp.pad(left.reshape(count, block, channels), ((0, 0), (0, eye_rows - block), (0, 0)))
        parts = [map_high, map_low, lefts, jnp.pad(bin_high, bin_pad), jnp.pad(bin_low, bin_pad)]
        parts = [jnp.broadcast_to(p, (count,) + p.shape[-2:]) for p in parts]
        return jnp.concatenate(parts, axis=1).transpose(0, 2, 1)

    turn = -core * (channels // 2)
    gain = jnp.broadcast_to(tri_gain[0][:, None], (channels, 2 * LANES))
    halved = w_tri * jnp.asarray(0.5, w_tri.dtype)
    right_w = jnp.concatenate([jnp.roll(halved[p].T, turn, axis=0) for p in (2, 3)], axis=0)
    left_w = jnp.concatenate(
        [jnp.roll(halved[p].T, turn, axis=0) for p in (0, 1)] + [halved[4].T], axis=0
    )
    cols = residue_index[None, :]

    block = 16 if local_rows % 16 == 0 else local_rows
    half_left = lax.dynamic_slice_in_dim(left_rows, half_start, half_rows, 0)
    half_index = lax.dynamic_slice_in_dim(residue_index, half_start, half_rows, 0)
    each = half_rows // CHUNKS
    kept, arriving = [], []
    r_block = 16 if each % 16 == 0 else each
    for n in range(CHUNKS):
        part = slice(n * each, (n + 1) * each)
        keep, send = edges(
            False,
            half_index[part],
            half_maps,
            mixing(half_left[part], r_block),
            right,
            gain,
            right_w,
            cols,
            r_block,
            n * each,
            each,
        )
        kept.append(keep)
        arriving.append(lax.ppermute(send, "mp", swap))
    left_keep, left_send, pair, gate = edges(
        True,
        lax.dynamic_slice_in_dim(residue_index, row_start, local_rows, 0),
        own_maps,
        mixing(lax.dynamic_slice_in_dim(left_rows, row_start, local_rows, 0), block),
        right,
        gain,
        left_w,
        cols,
        block,
    )
    lefts = jnp.concatenate([left_keep, lax.ppermute(left_send, "mp", swap)], axis=1)
    products = jnp.stack(
        [
            jnp.einsum("cik,cjk->cij", lefts, part, preferred_element_type=jnp.float32).astype(
                jnp.bfloat16
            )
            for part in kept + arriving
        ]
    )
    mine = products[:, :, :local_rows]
    theirs = lax.ppermute(products[:, :, local_rows:], "mp", swap)
    pair_out = finish(
        core[None],
        mine,
        theirs,
        pair,
        gate,
        jnp.broadcast_to(jnp.roll(tri_gain[1], turn)[:, None], (channels, each)),
        jnp.roll(w_tri_out, turn, axis=0).T,
        block,
    )
    return (hidden_out, pair_out)


def solution(mesh):
    placed = (
        P(("groups", "mp"), None),
        P(),
        P(None, None, "mp"),
        P("mp", None),
        P("groups"),
        P(),
        P(),
        P(),
        P(),
        P(),
        P(),
    )
    return jax.shard_map(
        per_device,
        mesh=mesh,
        in_specs=placed,
        out_specs=(P(("groups", "mp"), None), P(("groups", "mp"), None, None)),
        check_vma=False,
    )
```
